256 devices in a mesh: row: 16 (over z, x_lo), col: 8 (over x_hi, y), depth: 2 (over core).
Axes of the slice: x: 4 (x_hi: 2, x_lo: 2; x = x_hi * 2 + x_lo), y: 4, z: 8, core: 2. Of those that a mesh axis runs over, the one named last changes fastest.
Arguments:
- row_slab: bfloat16 [2048, 53248], P('row', ('col', 'depth')), may hold values from -6 to 6
- col_slab: bfloat16 [53248, 4096], P('row', ('col', 'depth')), may hold values from -0.046875 to 0.046875
- row_occupied: int32 [16, 416], P('row', ('col', 'depth')), may hold values 0 or 1
- col_occupied: int32 [416, 32], P('row', ('col', 'depth')), may hold values 0 or 1
- keep_mask: int32 [16, 32], P('row', ('col', 'depth')), may hold values 0 or 1
Outputs:
- squared: bfloat16 [2048, 4096], P('row', ('col', 'depth'))
The draws below stay inside these ranges and needn't reach their ends.
All inputs are finite; a program needn't handle non-finite values. No bound on the sum of `row_occupied` or of `col_occupied` or of `keep_mask` on one device may be relied on, other than what follows from the above.
Results may differ from the reference program's by a relative error of at most 0.001.
Values may be sent and summed in bfloat16 or wider, within the bound.
No kernel may reach another device: no remote copies, remote signals or barrier semaphores. Data moves between devices by JAX's collectives and lax.ppermute only.
A program may use at most 192 MiB of HBM per device.

```python
import jax
import jax.numpy as jnp

BLK = 128
N = 53248
ROWS = 2048
COLS = 4096


def plant(drawn, rng, low, largest):
    extent = drawn.shape
    index_at = [jax.random.randint(jax.random.fold_in(rng, axis), (), 0, extent[axis]) for axis in range(len(extent))]
    drawn = drawn.at[tuple(index_at)].set(low)
    longest = extent.index(max(extent))
    index_at[longest] = (index_at[longest] + 1) % extent[longest]
    return drawn.at[tuple(index_at)].set(largest)


def steps_of(key, dims, split, smallest, top_value):
    def one(dim, blocks):
        steps = jax.random.uniform(jax.random.fold_in(jax.random.fold_in(key, 6), dim), (blocks,), jnp.float32, smallest / len(split), top_value / len(split))
        return jnp.repeat(jnp.exp(steps), dims[dim] // blocks).reshape((-1,) + (1,) * (len(dims) - dim - 1))

    gain = one(*split[0])
    for cut in split[1:]:
        gain = gain * one(*cut)
    return gain


def noise(key, shape, spread, most, cuts=(), kind=jnp.bfloat16):
    gain = steps_of(key, shape, cuts, -0.22, 0.18) if cuts else 1.0
    values = jax.random.normal(key, shape, jnp.float32) * spread * gain
    return jnp.minimum(jnp.maximum(values, -most), most).astype(kind)


def setup_inputs(seed: int = 0) -> dict:
    arg_keys = jax.random.split(jax.random.key(seed), 6)
    row_slab = noise(arg_keys[0], (ROWS, N), 1.0, 6.0, ((0, 16), (1, 16)))
    col_slab = noise(arg_keys[1], (N, COLS), (N // 3) ** -0.5, 0.046875, ((0, 16), (1, 16)))
    row_occupied = plant((jax.random.randint(arg_keys[2], (ROWS // BLK, N // BLK), 0, 3) < 1).astype(jnp.int32), jax.random.fold_in(arg_keys[2], 1), 0, 1)
    col_occupied = plant((jax.random.randint(arg_keys[3], (N // BLK, COLS // BLK), 0, 3) < 1).astype(jnp.int32), jax.random.fold_in(arg_keys[3], 1), 0, 1)
    keep_mask = plant((jax.random.randint(arg_keys[4], (ROWS // BLK, COLS // BLK), 0, 4) < 3).astype(jnp.int32), jax.random.fold_in(arg_keys[4], 1), 0, 1)
    return {"row_slab": row_slab, "col_slab": col_slab, "row_occupied": row_occupied, "col_occupied": col_occupied, "keep_mask": keep_mask}


def masked(matrix, occupied):
    row_count = matrix.shape[0] // BLK
    col_count = matrix.shape[1] // BLK
    blocks = matrix.reshape(row_count, BLK, col_count, BLK) * occupied.astype(matrix.dtype)[:, None, :, None]
    return blocks.reshape(matrix.shape)


def reference(row_slab, col_slab, row_occupied, col_occupied, keep_mask):
    left_band = masked(row_slab, row_occupied)
    right_band = masked(col_slab, col_occupied)
    product = jnp.dot(left_band, right_band, preferred_element_type=jnp.float32)
    return masked(product, keep_mask).astype(jnp.bfloat16)
```

```python
import jax
import jax.numpy as jnp
from jax import lax
from jax.sharding import PartitionSpec as P

BLK = 128


def masked(matrix, occupied):
    row_count = matrix.shape[0] // BLK
    col_count = matrix.shape[1] // BLK
    blocks = (
        matrix.reshape(row_count, BLK, col_count, BLK)
        * occupied.astype(matrix.dtype)[:, None, :, None]
    )
    return blocks.reshape(matrix.shape)


def solution(mesh):
    rows = mesh.shape["row"]
    cols = mesh.shape["col"] * mesh.shape["depth"]
    turn = [(r * cols + c, c * cols + r) for r in range(rows) for c in range(cols)]

    def local(row_slab, col_slab, row_occupied, col_occupied, keep_mask):
        mine = masked(row_slab, row_occupied)
        right = masked(col_slab, col_occupied)
        turned = lax.ppermute(mine, ("row", "col", "depth"), turn)
        left = lax.all_gather(turned, ("col", "depth"), axis=0, tiled=True)
        partial = jnp.dot(left, right, preferred_element_type=jnp.float32)
        product = lax.psum_scatter(partial, "row", scatter_dimension=0, tiled=True)
        return masked(product, keep_mask).astype(jnp.bfloat16)

    spec = P("row", ("col", "depth"))
    return jax.shard_map(
        local, mesh=mesh, in_specs=(spec,) * 5, out_specs=spec, check_vma=False
    )
```

```python
import jax
import jax.numpy as jnp
from jax import lax
from jax.sharding import PartitionSpec as P

BLK = 128
AXES = ("row", "col", "depth")


def masked(matrix, occupied):
    row_count = matrix.shape[0] // BLK
    col_count = matrix.shape[1] // BLK
    blocks = (
        matrix.reshape(row_count, BLK, col_count, BLK)
        * occupied.astype(matrix.dtype)[:, None, :, None]
    )
    return blocks.reshape(matrix.shape)


def device(z, xl, xh, y, d):
    return (z * 2 + xl) * 16 + (xh * 4 + y) * 2 + d


def turn(t):
    return [
        (device(z, xl, xh, y, d), device(4 * xh + y, d, t ^ (z >> 2), (y - z + 2 * t + d) % 4, xl))
        for z in range(8)
        for xl in range(2)
        for xh in range(2)
        for y in range(4)
        for d in range(2)
    ]


def step_y(s):
    return [(xh * 4 + y, xh * 4 + (y + s) % 4) for xh in range(2) for y in range(4)]


SWAP_X = [(i, (i + 4) % 8) for i in range(8)]
SWAP_D = [(0, 1), (1, 0)]


def local(row_slab, col_slab, row_occupied, col_occupied, keep_mask):
    r, c, d = (lax.axis_index(a) for a in AXES)
    z, xl, xh, y = r // 2, r % 2, c // 4, c % 4
    half = row_slab.shape[0] // 2
    width = col_slab.shape[1]

    mine = masked(row_slab, row_occupied)
    own = []
    for t in range(2):
        part = lax.dynamic_slice_in_dim(mine, (t ^ (z // 4)) * half, half, 0)
        own.append(lax.ppermute(part, AXES, turn(t)))
    right = masked(col_slab, col_occupied)
    right = jnp.concatenate([right, lax.ppermute(right, "col", SWAP_X)], axis=1)

    up = [lax.ppermute(p, "col", step_y(1)) for p in own]
    down = [lax.ppermute(p, "col", step_y(-1)) for p in own]
    far = [lax.ppermute(up[0], "col", step_y(1)), lax.ppermute(down[1], "col", step_y(-1))]

    base = z - y + xl + 8
    partial = jnp.zeros((16, half, 2 * width), jnp.float32)
    for group in (
        [(t, 0, own[t]) for t in range(2)],
        [(t, j, p[t]) for j, p in ((1, up), (3, down)) for t in range(2)],
        [(t, 2, far[t]) for t in range(2)],
    ):
        pieces = [p for _, _, p in group] + [lax.ppermute(p, "depth", SWAP_D) for _, _, p in group]
        product = jnp.dot(
            jnp.concatenate(pieces, axis=0), right, preferred_element_type=jnp.float32
        ).reshape(len(pieces), half, 2 * width)
        for i in range(len(pieces)):
            t, j, _ = group[i % len(group)]
            source_xl = d if i < len(group) else 1 - d
            block = ((xh ^ t) * 4 + (base + 2 * t + j) % 4) * 2 + source_xl
            partial = lax.dynamic_update_slice(partial, product[i : i + 1], (block, 0, 0))

    total = jnp.sum(lax.all_to_all(partial, "row", 0, 0), axis=0).astype(jnp.bfloat16)
    kept, other = total[:, :width], lax.ppermute(total[:, width:], "col", SWAP_X)
    whole = jnp.where(
        xh == 0, jnp.concatenate([kept, other], 0), jnp.concatenate([other, kept], 0)
    )
    return masked(whole, keep_mask)


def solution(mesh):
    spec = P("row", ("col", "depth"))
    return jax.shard_map(
        local, mesh=mesh, in_specs=(spec,) * 5, out_specs=spec, check_vma=False
    )
```

```python
import jax
import jax.numpy as jnp
from jax import lax
from jax.sharding import PartitionSpec as P

BLK = 128
AXES = ("row", "col", "depth")


def masked(matrix, occupied):
    row_count = matrix.shape[0] // BLK
    col_count = matrix.shape[1] // BLK
    blocks = (
        matrix.reshape(row_count, BLK, col_count, BLK)
        * occupied.astype(matrix.dtype)[:, None, :, None]
    )
    return blocks.reshape(matrix.shape)


PLACES = [
    (z, xl, xh, y, d)
    for z in range(8)
    for xl in range(2)
    for xh in range(2)
    for y in range(4)
    for d in range(2)
]


def pairs(move):
    found = [(PLACES.index(p), PLACES.index(move(*p))) for p in PLACES]
    assert len({b for _, b in found}) == len(PLACES)
    return found


def in_plane(t):
    def move(z, xl, xh, y, d):
        s = (4 * xh + y - z - 4 * t - 2 * xl - d) % 8
        return z, d, s // 4, s % 4, xl

    return move


def along_z(t, way):
    def move(z, xl, xh, y, d):
        return (z + way * (4 * xh + y + 4 * t + 2 * d + xl)) % 8, xl, xh, y, d

    return move


def along_y(s):
    return lambda z, xl, xh, y, d: (z, xl, xh, (y + s) % 4, d)


def back(t, j):
    def move(z, xl, xh, y, d):
        there = along_z(t, -1)(z, xl, xh, (y - j) % 4, d)
        return there[0], xl, xh, y, d

    return move


def last(u, v):
    return lambda z, xl, xh, y, d: (z, d, u ^ xh, y, v ^ xl)


def send(x, move):
    return lax.ppermute(x, AXES, pairs(move))


def local(row_slab, col_slab, row_occupied, col_occupied, keep_mask):
    r, c, d = (lax.axis_index(a) for a in AXES)
    z, xl, xh, y = r // 2, r % 2, c // 4, c % 4
    half = row_slab.shape[0] // 2
    width = col_slab.shape[1]

    right = masked(col_slab, col_occupied)
    across_x = send(right, lambda z, xl, xh, y, d: (z, xl, 1 - xh, y, d))
    across_d = send(right, lambda z, xl, xh, y, d: (z, xl, xh, y, 1 - d))

    mine = masked(row_slab, row_occupied)
    parts = []
    for t in range(2):
        h = ((4 * xh + y - z - 4 * t - 2 * xl - d + 16) % 8) // 4
        parts.append(lax.dynamic_slice_in_dim(mine, h * half, half, 0))
    hop = lax.optimization_barrier([send(p, in_plane(t)) for t, p in enumerate(parts)])
    own = [send(p, along_z(t, 1)) for t, p in enumerate(hop)]
    up = [send(p, along_y(1)) for p in own]
    down = [send(p, along_y(-1)) for p in own]
    across_x, _ = lax.optimization_barrier((across_x, own))
    across_both = send(across_x, lambda z, xl, xh, y, d: (z, xl, xh, y, 1 - d))
    right = jnp.concatenate([right, across_x, across_d, across_both], axis=1)
    far = [send(up[0], along_y(1)), send(down[1], along_y(-1))]

    came = []
    for group in (
        [(t, 0, own[t]) for t in range(2)],
        [(t, 1, up[t]) for t in range(2)] + [(t, 3, down[t]) for t in range(2)],
        [(t, 2, far[t]) for t in range(2)],
    ):
        product = jnp.dot(
            jnp.concatenate([p for _, _, p in group], axis=0),
            right,
            preferred_element_type=jnp.float32,
        )
        for i, (t, j, _) in enumerate(group):
            came.append(send(product[i * half : (i + 1) * half], back(t, j)))
    total = sum(came[1:], came[0])

    halves = []
    for u in range(2):
        got = []
        for v in range(2):
            other_d = (v ^ xl) ^ d
            pick = lax.dynamic_slice_in_dim(total, (2 * other_d + u) * width, width, 1)
            got.append(send(pick, last(u, v)))
        halves.append(got[0] + got[1])
    whole = jnp.where(
        xh == 0,
        jnp.concatenate(halves, 0),
        jnp.concatenate(halves[::-1], 0),
    )
    return masked(whole, keep_mask).astype(jnp.bfloat16)


def solution(mesh):
    spec = P("row", ("col", "depth"))
    return jax.shard_map(
        local, mesh=mesh, in_specs=(spec,) * 5, out_specs=spec, check_vma=False
    )
```
